128 devices in a mesh: gx: 8 (over x, y_hi), gy: 16 (over z, y_lo, core).
Axes of the slice: x: 4, y: 4 (y_hi: 2, y_lo: 2; y = y_hi * 2 + y_lo), z: 4, core: 2. Of those that a mesh axis runs over, the one named last changes fastest.
Arguments:
- probes: float32 [48, 96, 64, 128], P('gx', 'gy'), may hold values from -6 to 6
- pair_blocks: float32 [48, 96, 9, 128, 128], P('gx', 'gy'), may hold values from -0.09375 to 0.09375
- partners: int32 [48, 96, 9], P('gx', 'gy'), may hold values from 0 to 4607, as said below
- shifts: int32 [2, 48, 96, 9], P(None, 'gx', 'gy'), may hold values from -1 to 1, as said below
- counts: int32 [48, 96], P('gx', 'gy'), may hold values from 1 to 9, as said below
- kpoint: float32 [2], replicated, may hold values from -3.140625 to 3.140625
Outputs:
- last_vector: float32 [48, 96, 64, 128], P('gx', 'gy')
- intersections: float32 [3, 2, 32], replicated
The draws below stay inside these ranges and needn't reach their ends.
Inputs may be any that keep to these rules, and one draw needn't show every extreme that they name: `partners`: slot 0 of cell (x, y) names the cell itself; slots 1 to 8 name its eight neighbouring cells (x + dx, y + dy) with dx, dy in -1..1 taken periodically modulo 48 and 96, each once, in no fixed order. shifts[0, x, y, s] = (x + dx - px) / 48 and shifts[1, x, y, s] = (y + dy - py) / 96 for the slot's offset (dx, dy) and partner cell (px, py). `counts`: slots at or beyond a cell's count are padding; some cell has all 9 slots live.
All inputs are finite; a program needn't handle non-finite values.
Results may differ from the reference program's by a relative error of at most 0.0001.
Values sent between devices are 32-bit elements; how exact they have to be, the bound alone decides.
No kernel may reach another device: no remote copies, remote signals or barrier semaphores. Data moves between devices by JAX's collectives and lax.ppermute only.
A program may use at most 128 MiB of HBM per device.

```python
import math
import jax
import jax.numpy as jnp
from jax import lax

CX = 6
CY = 6
BLOCK = 128
SLOTS = 9
PROBES = 32
STEPS = 3
NCX = 48
NCY = 96
ROWS = 589824


def pair_layout(key):
    base = jax.random.fold_in(key, 7)
    first_key, second_key, third_key = jax.random.split(base, 3)
    bricks_x = NCX // CX
    bricks_y = NCY // CY
    dense_brick = jax.random.randint(first_key, (bricks_x, bricks_y), 0, 2)
    dense_brick = dense_brick.at[0, 0].set(1)
    cell_x = jnp.arange(NCX, dtype=jnp.int32)[:, None]
    cell_y = jnp.arange(NCY, dtype=jnp.int32)[None, :]
    dense = dense_brick[cell_x // CX, cell_y // CY]
    live = jax.random.randint(second_key, (NCX, NCY, 8), 0, 2)
    live = jnp.maximum(live, dense[:, :, None])
    scores = jax.random.randint(third_key, (NCX, NCY, 8), 0, 1 << 20) * 8 + jnp.arange(8, dtype=jnp.int32)
    ranking = (1 - live) * (1 << 24) + scores
    order = jnp.argsort(ranking, axis=-1, stable=True).astype(jnp.int32)
    table_x = jnp.array([-1, -1, -1, 0, 0, 1, 1, 1], jnp.int32)
    table_y = jnp.array([-1, 0, 1, -1, 1, -1, 0, 1], jnp.int32)
    offset_x = jnp.take(table_x, order)
    offset_y = jnp.take(table_y, order)
    zero = jnp.zeros((NCX, NCY, 1), jnp.int32)
    offset_x = jnp.concatenate([zero, offset_x], axis=-1)
    offset_y = jnp.concatenate([zero, offset_y], axis=-1)
    target_x = cell_x[:, :, None] + offset_x
    target_y = cell_y[:, :, None] + offset_y
    partner_x = jnp.mod(target_x, NCX)
    partner_y = jnp.mod(target_y, NCY)
    shift_x = jnp.floor_divide(target_x, NCX)
    shift_y = jnp.floor_divide(target_y, NCY)
    partners = (partner_x * NCY + partner_y).astype(jnp.int32)
    shifts = jnp.stack([shift_x, shift_y]).astype(jnp.int32)
    counts = (1 + jnp.sum(live, axis=-1)).astype(jnp.int32)
    return (partners, shifts, counts)


def draw_partners(key, part):
    return pair_layout(key)[0]


def draw_shifts(key, part):
    return pair_layout(key)[1]


def draw_counts(key, part):
    return pair_layout(key)[2]


def block_levels(stream_key, extent, cuts, least, high):
    factor_of, own = 1.0, jax.random.fold_in(stream_key, 6)
    for position, parts in cuts:
        steps = jnp.exp(jax.random.uniform(jax.random.fold_in(own, position), (parts,), jnp.float32, least / len(cuts), high / len(cuts)))
        factor_of = factor_of * jnp.repeat(steps, extent[position] // parts).reshape([-1 if axis == position else 1 for axis in range(len(extent))])
    return factor_of


def gaussian(own_key, shape, spread, bound, shards=(), kind=jnp.bfloat16):
    gain = block_levels(own_key, shape, shards, -0.22, 0.18) if shards else 1.0
    drawn = jax.random.normal(own_key, shape, jnp.float32) * spread * gain
    return jnp.minimum(jnp.maximum(drawn, -bound), bound).astype(kind)


def setup_inputs(seed: int = 0) -> dict:
    arg_keys = jax.random.split(jax.random.key(seed), 7)
    probes = gaussian(arg_keys[0], (NCX, NCY, 2 * PROBES, BLOCK), 1.0, 6.0, ((0, 8), (1, 16)), jnp.float32)
    pair_blocks = gaussian(arg_keys[1], (NCX, NCY, SLOTS, BLOCK, BLOCK), (4 * BLOCK * SLOTS) ** -0.5, 0.09375, ((0, 8), (1, 16)), jnp.float32)
    partners = draw_partners(jax.random.fold_in(arg_keys[6], 71), 0)
    shifts = draw_shifts(jax.random.fold_in(arg_keys[6], 71), 0)
    counts = draw_counts(jax.random.fold_in(arg_keys[6], 71), 0)
    kpoint = jnp.clip(jax.random.uniform(arg_keys[5], (2,), jnp.float32, -3.140625, 3.140625), -3.140625, 3.140625)
    return dict(probes=probes, pair_blocks=pair_blocks, partners=partners, shifts=shifts, counts=counts, kpoint=kpoint)


def apply_hamiltonian(field, blocks, flat_partner, cosine, sine):
    cells = flat_partner.shape[0]
    width = field.shape[2]
    half = width // 2
    source = field.reshape(cells, width, BLOCK)

    def accumulate(slot, sums):
        real_sum, imag_sum = sums
        piece = jnp.take(source, flat_partner[:, slot], axis=0)
        block = lax.dynamic_index_in_dim(blocks, slot, 1, keepdims=False)
        product = jnp.einsum('npb,nba->npa', piece, block, precision=lax.Precision.HIGHEST)
        cos_part = lax.dynamic_index_in_dim(cosine, slot, 1, keepdims=False)[:, None, None]
        sin_part = lax.dynamic_index_in_dim(sine, slot, 1, keepdims=False)[:, None, None]
        real_part = product[:, :half]
        imag_part = product[:, half:]
        return (real_sum + cos_part * real_part - sin_part * imag_part, imag_sum + sin_part * real_part + cos_part * imag_part)
    zeros = jnp.zeros((cells, half, BLOCK), jnp.float32)
    real_sum, imag_sum = lax.fori_loop(0, SLOTS, accumulate, (zeros, zeros))
    return jnp.concatenate([real_sum, imag_sum], axis=1).reshape(field.shape)

def intersection(first, other):
    half = first.shape[2] // 2
    first_re, first_im = (first[:, :, :half], first[:, :, half:])
    other_re, other_im = (other[:, :, :half], other[:, :, half:])
    real_part = lax.optimization_barrier(jnp.sum(first_re * other_re + first_im * other_im, axis=(0, 1, 3)))
    imag_part = lax.optimization_barrier(jnp.sum(first_re * other_im - first_im * other_re, axis=(0, 1, 3)))
    return jnp.stack([real_part, imag_part])

def reference(probes, pair_blocks, partners, shifts, counts, kpoint):
    cells = NCX * NCY
    flat_partner = partners.reshape(cells, SLOTS).astype(jnp.int32)
    angle = kpoint[0] * shifts[0].astype(jnp.float32) + kpoint[1] * shifts[1].astype(jnp.float32)
    angle = angle.reshape(cells, SLOTS)
    live = (jnp.arange(SLOTS, dtype=jnp.int32)[None, :] < counts.reshape(cells, 1)).astype(jnp.float32)
    cosine = jnp.cos(angle) * live
    sine = jnp.sin(angle) * live
    blocks = pair_blocks.reshape(cells, SLOTS, BLOCK, BLOCK)
    scale = 1.0 / math.sqrt(ROWS)
    before = probes
    current = apply_hamiltonian(probes, blocks, flat_partner, cosine, sine)
    found = [intersection(probes, current) * scale]
    for step in range(STEPS - 1):
        following = 2.0 * apply_hamiltonian(current, blocks, flat_partner, cosine, sine) - before
        before, current = (current, following)
        found.append(intersection(probes, current) * scale)
    return (current, jnp.stack(found))
```

```python
import math

import jax
import jax.numpy as jnp
from jax import lax
from jax.experimental import pallas as pl
from jax.experimental.pallas import tpu as pltpu
from jax.sharding import PartitionSpec as P

AXES = ("gx", "gy")
F32 = jnp.float32
BF16 = jnp.bfloat16
VMEM = pl.BlockSpec(memory_space=pltpu.VMEM)
SMEM = pl.BlockSpec(memory_space=pltpu.SMEM)


def split_kernel(sizes, shape, kpoint, partners, counts, source, out, turn, blocks, arrived):
    cells_x, cells_y = shape
    total_x, total_y = sizes[0] * cells_x, sizes[1] * cells_y
    cells, slots, block, _ = blocks.shape
    loads = [pltpu.make_async_copy(source.at[i], blocks.at[i], arrived.at[i]) for i in range(cells)]
    for load in loads:
        load.start()
    me_x, me_y = lax.axis_index("gx"), lax.axis_index("gy")

    reach = 20
    scale = -(-(1 << reach) // total_y)
    assert all(p * scale >> reach == p // total_y for p in range(total_x * total_y))

    def offset(place, start, total):
        step = place - start + 1
        return jnp.where(step < 0, step + total, jnp.where(step > 2, step - total, step))

    def body(i, carry):
        x, y = i // cells_y, i % cells_y
        pltpu.make_async_copy(source.at[i], blocks.at[i], arrived.at[i]).wait()
        live = counts[x, y]
        for s in range(slots):
            partner = partners[x, y, s]
            place_x = lax.shift_right_logical(partner * scale, reach)
            along_x = offset(place_x, me_x * cells_x + x, total_x)
            along_y = offset(partner - place_x * total_y, me_y * cells_y + y, total_y)
            row = pl.multiple_of((along_x * 3 + along_y) * block, block)
            value = jnp.where(s < live, blocks[i, s], 0.0)
            high = value.astype(BF16)
            out[i, pl.ds(row, block), 0:block] = high
            out[i, pl.ds(row, block), block : 2 * block] = (value - high.astype(F32)).astype(BF16)
        return carry

    lax.fori_loop(0, cells, body, 0)

    wrap_left = jnp.where(me_x == 0, -1.0, 0.0)
    wrap_right = jnp.where(me_x == sizes[0] - 1, 1.0, 0.0)
    wrap_low = jnp.where(me_y == 0, -1.0, 0.0)
    wrap_high = jnp.where(me_y == sizes[1] - 1, 1.0, 0.0)
    wrap_outer = jnp.where(me_y % 2 == 1, wrap_high, wrap_low)
    zero = jnp.zeros_like(wrap_outer)
    sides = [(wrap_left, zero), (wrap_right, zero), (zero, wrap_outer)]
    sides += [(wrap_left, wrap_outer), (wrap_right, wrap_outer)]
    for k, (along_x, along_y) in enumerate(sides):
        angle = jnp.full(turn.shape[1:], kpoint[0] * along_x + kpoint[1] * along_y, F32)
        turn[2 * k] = jnp.cos(angle)
        turn[2 * k + 1] = jnp.sin(angle)


def put(ext, x, y, value):
    rows, block = value.shape
    high = value.astype(BF16)
    lanes = pl.ds(pl.multiple_of(y * block, block), block)
    ext[x, 0:rows, lanes] = high
    ext[x, rows : 2 * rows, lanes] = (value - high.astype(F32)).astype(BF16)


def turned(value, cos, sin):
    half = value.shape[0] // 2
    re, im = value[:half], value[half:]
    return jnp.concatenate([cos * re - sin * im, sin * re + cos * im], axis=0)


def apply_cell(ext, blocks, x, y, cells_y):
    block = blocks.shape[2] // 2
    rows = ext.shape[1] // 2
    lanes = pl.ds(pl.multiple_of(y * block, block), 3 * block)
    left = jnp.concatenate([ext[x + d, :, lanes] for d in range(3)], axis=1)
    full = jnp.dot(left, blocks[x * cells_y + y], preferred_element_type=F32)
    return (full[rows:, block:] + full[rows:, :block]) + (full[:rows, block:] + full[:rows, :block])


def update(first, ext, blocks, probes, before, new, at, sums, x, y, cells_y):
    i = x * cells_y + y
    value = apply_cell(ext, blocks, x, y, cells_y)
    if not first:
        value = 2.0 * value - before[i]
    new[at(i)] = value
    half = value.shape[0] // 2
    start = probes[i]
    sums[0] += start[:half] * value[:half] + start[half:] * value[half:]
    sums[1] += start[:half] * value[half:] - start[half:] * value[:half]
    return value


def inner_kernel(first, shape, field, blocks, probes, before, new, sums, ext):
    cells_x, cells_y = shape
    for x in range(cells_x):
        for y in range(cells_y):
            put(ext, x + 1, y + 1, field[x * cells_y + y])
    sums[...] = jnp.zeros_like(sums)
    width = cells_y - 2

    def body(k, carry):
        update(
            first, ext, blocks, probes, before, new, lambda i: k, sums, 1 + k // width, 1 + k % width, cells_y
        )
        return carry

    lax.fori_loop(0, (cells_x - 2) * width, body, 0, unroll=4)


def rim_kernel(
    first, shape, turn, field, blocks, probes, before, inner, inner_sums,
    left, right, outer, low, high, close,
    new, sums, e_left, e_right, e_outer, e_low, e_high, e_close, ext,
):
    cells_x, cells_y = shape
    odd = lax.axis_index("gy") % 2
    y_outer, y_close = odd * (cells_y + 1), (1 - odd) * (cells_y + 1)
    for x in range(cells_x):
        for y in range(cells_y):
            put(ext, x + 1, y + 1, field[x * cells_y + y])
    for y in range(cells_y):
        put(ext, 0, y + 1, turned(left[y], turn[0], turn[1]))
        put(ext, cells_x + 1, y + 1, turned(right[y], turn[2], turn[3]))
    for x in range(cells_x):
        put(ext, x + 1, y_outer, turned(outer[x], turn[4], turn[5]))
        put(ext, x + 1, y_close, close[x])
    put(ext, 0, y_outer, turned(low[0], turn[6], turn[7]))
    put(ext, cells_x + 1, y_outer, turned(high[0], turn[8], turn[9]))
    put(ext, 0, y_close, turned(close[cells_x], turn[0], turn[1]))
    put(ext, cells_x + 1, y_close, turned(close[cells_x + 1], turn[2], turn[3]))
    sums[...] = inner_sums[...]
    width = cells_y - 2
    for k in range((cells_x - 2) * width):
        new[(1 + k // width) * cells_y + 1 + k % width] = inner[k]

    def body(k, carry):
        across = k < 2 * cells_y
        rest = k - 2 * cells_y
        x = jnp.where(across, (k // cells_y) * (cells_x - 1), 1 + rest // 2)
        y = jnp.where(across, k % cells_y, (rest % 2) * (cells_y - 1))
        update(first, ext, blocks, probes, before, new, lambda i: i, sums, x, y, cells_y)
        return carry

    lax.fori_loop(0, 2 * cells_y + 2 * (cells_x - 2), body, 0, unroll=5)
    edges(shape, odd, new, e_left, e_right, e_outer, e_low, e_high, e_close)


def edges(shape, odd, field, e_left, e_right, e_outer, e_low, e_high, e_close):
    cells_x, cells_y = shape
    last = (cells_x - 1) * cells_y
    c_outer, c_close = odd * (cells_y - 1), (1 - odd) * (cells_y - 1)
    for y in range(cells_y):
        e_left[y] = field[last + y]
        e_right[y] = field[y]
    for x in range(cells_x):
        e_outer[x] = field[x * cells_y + c_outer]
        e_close[x] = field[x * cells_y + c_close]
    e_low[0] = field[last + c_outer]
    e_high[0] = field[c_outer]


def edge_kernel(shape, field, *outs):
    edges(shape, lax.axis_index("gy") % 2, field, *outs)


def corner_kernel(left, right, outer, low, high, close, done, out):
    near = (1 - lax.axis_index("gy") % 2) * (left.shape[0] - 1)
    cells_x = close.shape[0]
    for x in range(cells_x):
        out[x] = close[x]
    out[cells_x] = left[near]
    out[cells_x + 1] = right[near]


def pack_kernel(scale, first, second, third, out):
    terms = jnp.concatenate([r[k] for r in (first, second, third) for k in range(2)], axis=0)
    ones = jnp.full((8, terms.shape[1]), scale, F32)
    row = lax.dot_general(
        ones, terms, (((1,), (1,)), ((), ())), precision=lax.Precision.HIGHEST, preferred_element_type=F32
    )
    lanes = out.shape[2]
    row = jnp.concatenate([row, jnp.zeros((8, 2 * lanes - row.shape[1]), F32)], axis=1)
    out[:, 0, :] = jnp.broadcast_to(row[0:1, :lanes], (out.shape[0], lanes))
    out[:, 1, :] = jnp.broadcast_to(row[0:1, lanes:], (out.shape[0], lanes))


def params(mib):
    return pltpu.CompilerParams(vmem_limit_bytes=mib << 20)


def shards(sizes, probes, pair_blocks, partners, shifts, counts, kpoint):
    size_x, size_y = sizes
    cells_x, cells_y, width, block = probes.shape
    shape = (cells_x, cells_y)
    slots = pair_blocks.shape[2]
    cells = cells_x * cells_y
    half = width // 2
    total_x, total_y = cells_x * size_x, cells_y * size_y
    def table(move):
        pairs = []
        for i in range(size_x):
            for j in range(size_y):
                a, b = move(i, j)
                pairs.append((i * size_y + j, (a % size_x) * size_y + b % size_y))
        return pairs

    def over(j):
        return j + 1 if j % 2 else j - 1

    moves = dict(
        left=table(lambda i, j: (i + 1, j)),
        right=table(lambda i, j: (i - 1, j)),
        outer=table(lambda i, j: (i, over(j))),
        low=table(lambda i, j: (i + 1, over(j))),
        high=table(lambda i, j: (i - 1, over(j))),
    )

    field = probes.reshape(cells, width, block)
    raw = pair_blocks.reshape(cells, slots, block, block)
    cell = (width, block)
    edge_shapes = [
        jax.ShapeDtypeStruct((n,) + cell, F32) for n in (cells_y, cells_y, cells_x, 1, 1, cells_x)
    ]
    field_shape = jax.ShapeDtypeStruct((cells,) + cell, F32)
    inner_shape = jax.ShapeDtypeStruct(((cells_x - 2) * (cells_y - 2),) + cell, F32)
    sums_shape = jax.ShapeDtypeStruct((2, half, block), F32)
    scratch = [pltpu.VMEM((cells_x + 2, 2 * width, (cells_y + 2) * block), BF16)]

    sides = pl.pallas_call(
        lambda *r: edge_kernel(shape, *r),
        out_shape=edge_shapes, in_specs=[VMEM], out_specs=[VMEM] * 6,
        compiler_params=params(1), name="edges",
    )(field)

    blocks, turn = pl.pallas_call(
        lambda *r: split_kernel(sizes, shape, *r),
        out_shape=[
            jax.ShapeDtypeStruct((cells, slots * block, 2 * block), BF16),
            jax.ShapeDtypeStruct((10, half, block), F32),
        ],
        in_specs=[SMEM, SMEM, SMEM, pl.BlockSpec(memory_space=pl.ANY)], out_specs=[VMEM] * 2,
        scratch_shapes=[pltpu.VMEM(raw.shape, F32), pltpu.SemaphoreType.DMA((cells,))],
        compiler_params=params(22), name="split",
        cost_estimate=pl.CostEstimate(flops=4 * raw.size, bytes_accessed=8 * raw.size, transcendentals=0),
    )(kpoint, partners, counts, pltpu.with_memory_space_constraint(raw, pltpu.HBM))

    flops = 8 * width * block * block * slots

    def step(first, field, before, sides):
        *sides, close = sides
        halo = [lax.ppermute(s, AXES, moves[n]) for n, s in zip(names, sides)]
        inner, inner_sums = pl.pallas_call(
            lambda *r: inner_kernel(first, shape, *r),
            out_shape=[inner_shape, sums_shape], in_specs=[VMEM] * 4, out_specs=[VMEM] * 2,
            scratch_shapes=scratch, compiler_params=params(6), name="inner",
            cost_estimate=pl.CostEstimate(flops=16 * flops, bytes_accessed=0, transcendentals=0),
        )(field, blocks, probes_flat, before)
        close = pl.pallas_call(
            corner_kernel, out_shape=jax.ShapeDtypeStruct((cells_x + 2,) + cell, F32),
            in_specs=[VMEM] * 7, out_specs=VMEM, compiler_params=params(1), name="corner",
        )(*halo, close, inner_sums)
        close = lax.ppermute(close, AXES, table(lambda i, j: (i, j ^ 1)))
        out = pl.pallas_call(
            lambda *r: rim_kernel(first, shape, *r),
            out_shape=[field_shape, sums_shape] + edge_shapes,
            in_specs=[VMEM] * 13, out_specs=[VMEM] * 8,
            scratch_shapes=scratch, compiler_params=params(8), name="rim",
            cost_estimate=pl.CostEstimate(flops=20 * flops, bytes_accessed=0, transcendentals=0),
        )(turn, field, blocks, probes_flat, before, inner, inner_sums,
          *halo, close)
        return out[0], out[1], out[2:]

    probes_flat = field
    names = ("left", "right", "outer", "low", "high")
    before, found = field, []
    for n in range(3):
        new, sums, sides = step(n == 0, field, before, sides)
        found.append(sums)
        before, field = field, new

    scale = 1.0 / math.sqrt(total_x * total_y * block)
    spread = pl.pallas_call(
        lambda *r: pack_kernel(scale, *r),
        out_shape=jax.ShapeDtypeStruct((size_x * size_y, 2, 128), F32),
        in_specs=[VMEM] * 3, out_specs=VMEM, compiler_params=params(2), name="pack",
    )(*found)
    total = jnp.sum(lax.all_to_all(spread, AXES, 0, 0), axis=0).reshape(-1)
    total = total[: 3 * 2 * half].reshape(3, 2, half)
    return field.reshape(probes.shape), total


def solution(mesh):
    sizes = (mesh.shape["gx"], mesh.shape["gy"])
    placed = (
        P("gx", "gy", None, None),
        P("gx", "gy", None, None, None),
        P("gx", "gy", None),
        P(None, "gx", "gy", None),
        P("gx", "gy"),
        P(),
    )
    return jax.shard_map(
        lambda *a: shards(sizes, *a), mesh=mesh, in_specs=placed,
        out_specs=(P("gx", "gy", None, None), P()), check_vma=False,
    )
```

```python
import math

import jax
import jax.numpy as jnp
from jax import lax
from jax.experimental import pallas as pl
from jax.experimental.pallas import tpu as pltpu
from jax.sharding import PartitionSpec as P

AXES = ("gx", "gy")
F32 = jnp.float32
BF16 = jnp.bfloat16
VMEM = pl.BlockSpec(memory_space=pltpu.VMEM)
SMEM = pl.BlockSpec(memory_space=pltpu.SMEM)


def split_kernel(sizes, shape, kpoint, partners, counts, source, out, turn, blocks, arrived):
    cells_x, cells_y = shape
    total_x, total_y = sizes[0] * cells_x, sizes[1] * cells_y
    cells, slots, block, _ = blocks.shape
    loads = [pltpu.make_async_copy(source.at[i], blocks.at[i], arrived.at[i]) for i in range(cells)]
    for load in loads:
        load.start()
    me_x, me_y = lax.axis_index("gx"), lax.axis_index("gy")

    reach = 20
    scale = -(-(1 << reach) // total_y)
    assert all(p * scale >> reach == p // total_y for p in range(total_x * total_y))

    def offset(place, start, total):
        step = place - start + 1
        return jnp.where(step < 0, step + total, jnp.where(step > 2, step - total, step))

    def body(i, carry):
        x, y = i // cells_y, i % cells_y
        pltpu.make_async_copy(source.at[i], blocks.at[i], arrived.at[i]).wait()
        live = counts[x, y]
        for s in range(slots):
            partner = partners[x, y, s]
            place_x = lax.shift_right_logical(partner * scale, reach)
            along_x = offset(place_x, me_x * cells_x + x, total_x)
            along_y = offset(partner - place_x * total_y, me_y * cells_y + y, total_y)
            row = pl.multiple_of((along_x * 3 + along_y) * block, block)
            value = jnp.where(s < live, blocks[i, s], 0.0)
            high = value.astype(BF16)
            out[i, pl.ds(row, block), 0:block] = high
            out[i, pl.ds(row, block), block : 2 * block] = (value - high.astype(F32)).astype(BF16)
        return carry

    lax.fori_loop(0, cells, body, 0)

    wrap_left = jnp.where(me_x == 0, -1.0, 0.0)
    wrap_right = jnp.where(me_x == sizes[0] - 1, 1.0, 0.0)
    wrap_low = jnp.where(me_y == 0, -1.0, 0.0)
    wrap_high = jnp.where(me_y == sizes[1] - 1, 1.0, 0.0)
    wrap_outer = jnp.where(me_y % 2 == 1, wrap_high, wrap_low)
    zero = jnp.zeros_like(wrap_outer)
    sides = [(wrap_left, zero), (wrap_right, zero), (zero, wrap_outer)]
    sides += [(wrap_left, wrap_outer), (wrap_right, wrap_outer)]
    for k, (along_x, along_y) in enumerate(sides):
        angle = jnp.full(turn.shape[1:], kpoint[0] * along_x + kpoint[1] * along_y, F32)
        turn[2 * k] = jnp.cos(angle)
        turn[2 * k + 1] = jnp.sin(angle)


def put(ext, x, y, value):
    rows, block = value.shape
    high = value.astype(BF16)
    lanes = pl.ds(pl.multiple_of(y * block, block), block)
    ext[x, 0:rows, lanes] = high
    ext[x, rows : 2 * rows, lanes] = (value - high.astype(F32)).astype(BF16)


def turned(value, cos, sin):
    half = value.shape[0] // 2
    re, im = value[:half], value[half:]
    return jnp.concatenate([cos * re - sin * im, sin * re + cos * im], axis=0)


def fold(full, rows, block):
    return (full[rows:, block:] + full[rows:, :block]) + (full[:rows, block:] + full[:rows, :block])


def apply_cell(ext, blocks, x, y, cells_y):
    block = blocks.shape[2] // 2
    lanes = pl.ds(pl.multiple_of(y * block, block), 3 * block)
    left = jnp.concatenate([ext[x + d, :, lanes] for d in range(3)], axis=1)
    full = jnp.dot(left, blocks[x * cells_y + y], preferred_element_type=F32)
    return fold(full, ext.shape[1] // 2, block)


def apply_part(ext, blocks, x, y, shape, local):
    cells_x, cells_y = shape
    block = blocks.shape[2] // 2
    left, right = [], []
    for k in range(9):
        a, b = x + k // 3, y + k % 3
        if (1 <= a <= cells_x and 1 <= b <= cells_y) == local:
            left.append(ext[a, :, b * block : (b + 1) * block])
            right.append(blocks[x * cells_y + y, k * block : (k + 1) * block, :])
    full = jnp.dot(
        jnp.concatenate(left, axis=1), jnp.concatenate(right, axis=0), preferred_element_type=F32
    )
    return fold(full, ext.shape[1] // 2, block)


def rim_cells(shape):
    cells_x, cells_y = shape
    return [
        (x, y) for x in range(cells_x) for y in range(cells_y)
        if x in (0, cells_x - 1) or y in (0, cells_y - 1)
    ]


def terms(start, value):
    half = value.shape[0] // 2
    real = start[:half] * value[:half] + start[half:] * value[half:]
    return real, start[:half] * value[half:] - start[half:] * value[:half]


def put_field(ext, field, shape):
    cells_x, cells_y = shape
    for x in range(cells_x):
        for y in range(cells_y):
            put(ext, x + 1, y + 1, field[x * cells_y + y])


def inner_kernel(first, shape, field, blocks, probes, before, done, out, sums, ext):
    cells_x, cells_y = shape
    put_field(ext, field, shape)
    sums[...] = jnp.zeros_like(sums)
    width = cells_y - 2

    def body(k, carry):
        x, y = 1 + k // width, 1 + k % width
        i = x * cells_y + y
        value = apply_cell(ext, blocks, x, y, cells_y)
        if not first:
            value = 2.0 * value - before[i]
        out[k] = value
        real, imag = terms(probes[i], value)
        sums[0] += real
        sums[1] += imag
        return carry

    lax.fori_loop(0, (cells_x - 2) * width, body, 0, unroll=4)


def local_kernel(shape, field, blocks, done, out, ext):
    put_field(ext, field, shape)
    for k, (x, y) in enumerate(rim_cells(shape)):
        out[k] = apply_part(ext, blocks, x, y, shape, True)


def rim_kernel(
    first, shape, turn, blocks, probes, before, inner, inner_sums, local, left, right, outer, close, *rest
):
    cells_x, cells_y = shape
    if first:
        low, high = outer.at[cells_x], outer.at[cells_x + 1]
    else:
        low, high, *rest = rest
        low, high = low.at[0], high.at[0]
    new, sums, *sides, ext = rest
    odd = lax.axis_index("gy") % 2
    y_outer, y_close = odd * (cells_y + 1), (1 - odd) * (cells_y + 1)
    for y in range(cells_y):
        put(ext, 0, y + 1, turned(left[y], turn[0], turn[1]))
        put(ext, cells_x + 1, y + 1, turned(right[y], turn[2], turn[3]))
    for x in range(cells_x):
        put(ext, x + 1, y_outer, turned(outer[x], turn[4], turn[5]))
        put(ext, x + 1, y_close, close[x])
    put(ext, 0, y_outer, turned(low[...], turn[6], turn[7]))
    put(ext, cells_x + 1, y_outer, turned(high[...], turn[8], turn[9]))
    put(ext, 0, y_close, turned(close[cells_x], turn[0], turn[1]))
    put(ext, cells_x + 1, y_close, turned(close[cells_x + 1], turn[2], turn[3]))
    width = cells_y - 2
    for k in range((cells_x - 2) * width):
        new[(1 + k // width) * cells_y + 1 + k % width] = inner[k]
    real_sum, imag_sum = inner_sums[0], inner_sums[1]
    for k, (x, y) in enumerate(rim_cells(shape)):
        i = x * cells_y + y
        value = local[k] + apply_part(ext, blocks, x, y, shape, False)
        if not first:
            value = 2.0 * value - before[i]
        new[i] = value
        real, imag = terms(probes[i], value)
        real_sum, imag_sum = real_sum + real, imag_sum + imag
    sums[0] = real_sum
    sums[1] = imag_sum
    if sides:
        edges(shape, odd, new, *sides)


def edges(shape, odd, field, e_left, e_right, e_outer, e_low, e_high, e_close):
    cells_x, cells_y = shape
    last = (cells_x - 1) * cells_y
    c_outer, c_close = odd * (cells_y - 1), (1 - odd) * (cells_y - 1)
    for y in range(cells_y):
        e_left[y] = field[last + y]
        e_right[y] = field[y]
    for x in range(cells_x):
        e_outer[x] = field[x * cells_y + c_outer]
        e_close[x] = field[x * cells_y + c_close]
    e_low[0] = field[last + c_outer]
    e_high[0] = field[c_outer]


def edge_kernel(field, left, right, arrived):
    loads = [
        pltpu.make_async_copy(field.at[field.shape[0] - 1], left, arrived.at[0]),
        pltpu.make_async_copy(field.at[0], right, arrived.at[1]),
    ]
    for load in loads:
        load.start()
    for load in loads:
        load.wait()


def first_pack_kernel(shape, field, left, right, done, outer, close):
    cells_x, cells_y = shape
    odd = lax.axis_index("gy") % 2
    c_outer, c_close = odd * (cells_y - 1), (1 - odd) * (cells_y - 1)
    for out, c in ((outer, c_outer), (close, c_close)):
        for x in range(cells_x):
            out[x] = field[x * cells_y + c]
        out[cells_x] = left[c]
        out[cells_x + 1] = right[c]


def pack_close_kernel(left, right, outer, low, high, close, done, out):
    near = (1 - lax.axis_index("gy") % 2) * (left.shape[0] - 1)
    cells_x = close.shape[0]
    for x in range(cells_x):
        out[x] = close[x]
    out[cells_x] = left[near]
    out[cells_x + 1] = right[near]


def pack_kernel(scale, first, second, third, out):
    terms = jnp.concatenate([r[k] for r in (first, second, third) for k in range(2)], axis=0)
    ones = jnp.full((8, terms.shape[1]), scale, F32)
    row = lax.dot_general(
        ones, terms, (((1,), (1,)), ((), ())), precision=lax.Precision.HIGHEST, preferred_element_type=F32
    )
    lanes = out.shape[2]
    row = jnp.concatenate([row, jnp.zeros((8, 2 * lanes - row.shape[1]), F32)], axis=1)
    out[:, 0, :] = jnp.broadcast_to(row[0:1, :lanes], (out.shape[0], lanes))
    out[:, 1, :] = jnp.broadcast_to(row[0:1, lanes:], (out.shape[0], lanes))


def params(mib):
    return pltpu.CompilerParams(vmem_limit_bytes=mib << 20)


def shards(sizes, probes, pair_blocks, partners, shifts, counts, kpoint):
    size_x, size_y = sizes
    cells_x, cells_y, width, block = probes.shape
    shape = (cells_x, cells_y)
    slots = pair_blocks.shape[2]
    cells = cells_x * cells_y
    half = width // 2
    total_x, total_y = cells_x * size_x, cells_y * size_y
    def table(move):
        pairs = []
        for i in range(size_x):
            for j in range(size_y):
                a, b = move(i, j)
                pairs.append((i * size_y + j, (a % size_x) * size_y + b % size_y))
        return pairs

    def over(j):
        return j + 1 if j % 2 else j - 1

    moves = [
        table(lambda i, j: (i + 1, j)),
        table(lambda i, j: (i - 1, j)),
        table(lambda i, j: (i, over(j))),
        table(lambda i, j: (i + 1, over(j))),
        table(lambda i, j: (i - 1, over(j))),
    ]
    on_chip = table(lambda i, j: (i, j ^ 1))

    def send(value, move):
        return lax.ppermute(value, AXES, move)

    field = probes.reshape(cells, width, block)
    raw = pair_blocks.reshape(cells, slots, block, block)
    cell = (width, block)
    edge_shapes = [
        jax.ShapeDtypeStruct((n,) + cell, F32) for n in (cells_y, cells_y, cells_x, 1, 1, cells_x)
    ]
    field_shape = jax.ShapeDtypeStruct((cells,) + cell, F32)
    inner_shape = jax.ShapeDtypeStruct(((cells_x - 2) * (cells_y - 2),) + cell, F32)
    sums_shape = jax.ShapeDtypeStruct((2, half, block), F32)
    scratch = [pltpu.VMEM((cells_x + 2, 2 * width, (cells_y + 2) * block), BF16)]

    cells_shape = lambda n: jax.ShapeDtypeStruct((n,) + cell, F32)
    call = lambda body, ins, outs, mib, name, **more: pl.pallas_call(
        body, out_shape=outs, in_specs=[VMEM] * ins, out_specs=[VMEM] * len(outs),
        compiler_params=params(mib), name=name, **more,
    )
    sides = pl.pallas_call(
        edge_kernel,
        out_shape=[cells_shape(cells_y)] * 2,
        in_specs=[pl.BlockSpec(memory_space=pl.ANY)], out_specs=[VMEM] * 2,
        scratch_shapes=[pltpu.SemaphoreType.DMA((2,))],
        compiler_params=params(1), name="edges",
    )(pltpu.with_memory_space_constraint(probes.reshape(cells_x, cells_y, width, block), pltpu.HBM))

    blocks, turn = pl.pallas_call(
        lambda *r: split_kernel(sizes, shape, *r),
        out_shape=[
            jax.ShapeDtypeStruct((cells, slots * block, 2 * block), BF16),
            jax.ShapeDtypeStruct((10, half, block), F32),
        ],
        in_specs=[SMEM, SMEM, SMEM, pl.BlockSpec(memory_space=pl.ANY)], out_specs=[VMEM] * 2,
        scratch_shapes=[pltpu.VMEM(raw.shape, F32), pltpu.SemaphoreType.DMA((cells,))],
        compiler_params=params(22), name="split",
        cost_estimate=pl.CostEstimate(flops=4 * raw.size, bytes_accessed=8 * raw.size, transcendentals=0),
    )(kpoint, partners, counts, pltpu.with_memory_space_constraint(raw, pltpu.HBM))

    flops = 8 * width * block * block * slots

    rim = len(rim_cells(shape))

    def cost(cells):
        return pl.CostEstimate(flops=cells * flops, bytes_accessed=0, transcendentals=0)

    def inner(first, field, before, after):
        return call(
            lambda *r: inner_kernel(first, shape, *r), 5, [inner_shape, sums_shape], 6, "inner",
            scratch_shapes=scratch, cost_estimate=cost(16),
        )(field, blocks, probes_flat, before, after)

    def local(field, after):
        return call(
            lambda *r: local_kernel(shape, *r), 3, [cells_shape(rim)], 6, "local",
            scratch_shapes=scratch, cost_estimate=cost(12),
        )(field, blocks, after)

    def outside(first, last, before, parts, halo):
        outs = [field_shape, sums_shape] + ([] if last else edge_shapes)
        return call(
            lambda *r: rim_kernel(first, shape, *r), 7 + len(halo), outs, 6, "rim",
            scratch_shapes=scratch, cost_estimate=cost(8),
        )(turn, blocks, probes_flat, before, *parts, *halo)

    def first_step(field, sides):
        left, right = send(sides[0], moves[0]), send(sides[1], moves[1])
        outer, close = call(
            lambda *r: first_pack_kernel(shape, *r), 4, [cells_shape(cells_x + 2)] * 2, 1, "pack_sides"
        )(field, left, right, turn)
        after = outer
        outer, close = send(outer, moves[2]), send(close, on_chip)
        parts = [*inner(True, field, field, after), *local(field, after)]
        return outside(True, False, field, parts, [left, right, outer, close])

    def step(last, field, before, sides):
        *sides, close = sides
        halo = [send(s, m) for s, m in zip(sides, moves)]
        parts = inner(False, field, before, field)
        (close,) = call(
            pack_close_kernel, 7, [cells_shape(cells_x + 2)], 1, "pack_close"
        )(*halo, close, parts[1])
        after = close
        close = send(close, on_chip)
        parts = [*parts, *local(field, after)]
        left, right, outer, low, high = halo
        return outside(False, last, before, parts, [left, right, outer, close, low, high])

    probes_flat = field
    new, sums, *sides = first_step(field, sides)
    before, field, found = field, new, [sums]
    for n in range(1, 3):
        new, sums, *sides = step(n == 2, field, before, sides)
        before, field = field, new
        found.append(sums)

    scale = 1.0 / math.sqrt(total_x * total_y * block)
    spread = pl.pallas_call(
        lambda *r: pack_kernel(scale, *r),
        out_shape=jax.ShapeDtypeStruct((size_x * size_y, 2, 128), F32),
        in_specs=[VMEM] * 3, out_specs=VMEM, compiler_params=params(2), name="pack",
    )(*found)
    total = jnp.sum(lax.all_to_all(spread, AXES, 0, 0), axis=0).reshape(-1)
    total = total[: 3 * 2 * half].reshape(3, 2, half)
    return field.reshape(probes.shape), total


def solution(mesh):
    sizes = (mesh.shape["gx"], mesh.shape["gy"])
    placed = (
        P("gx", "gy", None, None),
        P("gx", "gy", None, None, None),
        P("gx", "gy", None),
        P(None, "gx", "gy", None),
        P("gx", "gy"),
        P(),
    )
    return jax.shard_map(
        lambda *a: shards(sizes, *a), mesh=mesh, in_specs=placed,
        out_specs=(P("gx", "gy", None, None), P()), check_vma=False,
    )
```

```python
import math

import jax
import jax.numpy as jnp
from jax import lax
from jax.experimental import pallas as pl
from jax.experimental.pallas import tpu as pltpu
from jax.sharding import PartitionSpec as P

AXES = ("gx", "gy")
F32 = jnp.float32
BF16 = jnp.bfloat16
VMEM = pl.BlockSpec(memory_space=pltpu.VMEM)
SMEM = pl.BlockSpec(memory_space=pltpu.SMEM)


def split_kernel(sizes, shape, kpoint, partners, counts, source, out, turn, blocks, arrived):
    cells_x, cells_y = shape
    total_x, total_y = sizes[0] * cells_x, sizes[1] * cells_y
    cells, slots, block, _ = blocks.shape
    loads = [pltpu.make_async_copy(source.at[i], blocks.at[i], arrived.at[i]) for i in range(cells)]
    for load in loads:
        load.start()
    me_x, me_y = lax.axis_index("gx"), lax.axis_index("gy")

    reach = 20
    scale = -(-(1 << reach) // total_y)
    assert all(p * scale >> reach == p // total_y for p in range(total_x * total_y))

    def offset(place, start, total):
        step = place - start + 1
        return jnp.where(step < 0, step + total, jnp.where(step > 2, step - total, step))

    def body(i, carry):
        x, y = i // cells_y, i % cells_y
        pltpu.make_async_copy(source.at[i], blocks.at[i], arrived.at[i]).wait()
        live = counts[x, y]
        for s in range(slots):
            partner = partners[x, y, s]
            place_x = lax.shift_right_logical(partner * scale, reach)
            along_x = offset(place_x, me_x * cells_x + x, total_x)
            along_y = offset(partner - place_x * total_y, me_y * cells_y + y, total_y)
            row = pl.multiple_of((along_x * 3 + along_y) * block, block)
            value = jnp.where(s < live, blocks[i, s], 0.0)
            high = value.astype(BF16)
            out[i, pl.ds(row, block), 0:block] = high
            out[i, pl.ds(row, block), block : 2 * block] = (value - high.astype(F32)).astype(BF16)
        return carry

    lax.fori_loop(0, cells, body, 0)

    wrap_left = jnp.where(me_x == 0, -1.0, 0.0)
    wrap_right = jnp.where(me_x == sizes[0] - 1, 1.0, 0.0)
    wrap_low = jnp.where(me_y == 0, -1.0, 0.0)
    wrap_high = jnp.where(me_y == sizes[1] - 1, 1.0, 0.0)
    wrap_outer = jnp.where(me_y % 2 == 1, wrap_high, wrap_low)
    zero = jnp.zeros_like(wrap_outer)
    sides = [(wrap_left, zero), (wrap_right, zero), (zero, wrap_outer)]
    sides += [(wrap_left, wrap_outer), (wrap_right, wrap_outer)]
    for k, (along_x, along_y) in enumerate(sides):
        angle = jnp.full(turn.shape[1:], kpoint[0] * along_x + kpoint[1] * along_y, F32)
        turn[2 * k] = jnp.cos(angle)
        turn[2 * k + 1] = jnp.sin(angle)


def put(ext, x, y, value):
    rows, block = value.shape
    high = value.astype(BF16)
    lanes = pl.ds(pl.multiple_of(y * block, block), block)
    ext[x, 0:rows, lanes] = high
    ext[x, rows : 2 * rows, lanes] = (value - high.astype(F32)).astype(BF16)


def turned(value, cos, sin):
    half = value.shape[0] // 2
    re, im = value[:half], value[half:]
    return jnp.concatenate([cos * re - sin * im, sin * re + cos * im], axis=0)


def fold(full, rows, block):
    return (full[rows:, block:] + full[rows:, :block]) + (full[:rows, block:] + full[:rows, :block])


def apply_cell(ext, blocks, x, y, cells_y):
    block = blocks.shape[2] // 2
    lanes = pl.ds(pl.multiple_of(y * block, block), 3 * block)
    left = jnp.concatenate([ext[x + d, :, lanes] for d in range(3)], axis=1)
    full = jnp.dot(left, blocks[x * cells_y + y], preferred_element_type=F32)
    return fold(full, ext.shape[1] // 2, block)


def apply_part(ext, blocks, x, y, shape, local):
    cells_x, cells_y = shape
    block = blocks.shape[2] // 2
    left, right = [], []
    for k in range(9):
        a, b = x + k // 3, y + k % 3
        if (1 <= a <= cells_x and 1 <= b <= cells_y) == local:
            left.append(ext[a, :, b * block : (b + 1) * block])
            right.append(blocks[x * cells_y + y, k * block : (k + 1) * block, :])
    full = jnp.dot(
        jnp.concatenate(left, axis=1), jnp.concatenate(right, axis=0), preferred_element_type=F32
    )
    return fold(full, ext.shape[1] // 2, block)


def rim_cells(shape):
    cells_x, cells_y = shape
    return [
        (x, y) for x in range(cells_x) for y in range(cells_y)
        if x in (0, cells_x - 1) or y in (0, cells_y - 1)
    ]


def terms(start, value):
    half = value.shape[0] // 2
    real = start[:half] * value[:half] + start[half:] * value[half:]
    return real, start[:half] * value[half:] - start[half:] * value[:half]


def put_field(ext, field, shape):
    cells_x, cells_y = shape
    for x in range(cells_x):
        for y in range(cells_y):
            put(ext, x + 1, y + 1, field[x * cells_y + y])


def inner_kernel(first, shape, field, blocks, probes, before, done, out, sums, ext):
    cells_x, cells_y = shape
    put_field(ext, field, shape)
    sums[...] = jnp.zeros_like(sums)
    width = cells_y - 2

    def body(k, carry):
        x, y = 1 + k // width, 1 + k % width
        i = x * cells_y + y
        value = apply_cell(ext, blocks, x, y, cells_y)
        if not first:
            value = 2.0 * value - before[i]
        out[k] = value
        real, imag = terms(probes[i], value)
        sums[0] += real
        sums[1] += imag
        return carry

    lax.fori_loop(0, (cells_x - 2) * width, body, 0, unroll=4)


def local_kernel(shape, field, blocks, done, out, ext):
    put_field(ext, field, shape)
    for k, (x, y) in enumerate(rim_cells(shape)):
        out[k] = apply_part(ext, blocks, x, y, shape, True)


def rim_kernel(
    first, shape, turn, blocks, probes, before, inner, inner_sums, local, left, right, outer, close, *rest
):
    cells_x, cells_y = shape
    if first:
        low, *rest = rest
        low, high = low.at[0], low.at[1]
    else:
        low, high, *rest = rest
        low, high = low.at[0], high.at[0]
    new, sums, *sides, ext = rest
    odd = lax.axis_index("gy") % 2
    y_outer, y_close = odd * (cells_y + 1), (1 - odd) * (cells_y + 1)
    for y in range(cells_y):
        put(ext, 0, y + 1, turned(left[y], turn[0], turn[1]))
        put(ext, cells_x + 1, y + 1, turned(right[y], turn[2], turn[3]))
    for x in range(cells_x):
        put(ext, x + 1, y_outer, turned(outer[x], turn[4], turn[5]))
        put(ext, x + 1, y_close, close[x])
    put(ext, 0, y_outer, turned(low[...], turn[6], turn[7]))
    put(ext, cells_x + 1, y_outer, turned(high[...], turn[8], turn[9]))
    put(ext, 0, y_close, turned(close[cells_x], turn[0], turn[1]))
    put(ext, cells_x + 1, y_close, turned(close[cells_x + 1], turn[2], turn[3]))
    width = cells_y - 2
    for k in range((cells_x - 2) * width):
        new[(1 + k // width) * cells_y + 1 + k % width] = inner[k]
    real_sum, imag_sum = inner_sums[0], inner_sums[1]
    for k, (x, y) in enumerate(rim_cells(shape)):
        i = x * cells_y + y
        value = local[k] + apply_part(ext, blocks, x, y, shape, False)
        if not first:
            value = 2.0 * value - before[i]
        new[i] = value
        real, imag = terms(probes[i], value)
        real_sum, imag_sum = real_sum + real, imag_sum + imag
    sums[0] = real_sum
    sums[1] = imag_sum
    if sides:
        edges(shape, odd, new, *sides)


def edges(shape, odd, field, e_left, e_right, e_outer, e_low, e_high, e_close):
    cells_x, cells_y = shape
    last = (cells_x - 1) * cells_y
    c_outer, c_close = odd * (cells_y - 1), (1 - odd) * (cells_y - 1)
    for y in range(cells_y):
        e_left[y] = field[last + y]
        e_right[y] = field[y]
    for x in range(cells_x):
        e_outer[x] = field[x * cells_y + c_outer]
        e_close[x] = field[x * cells_y + c_close]
    e_low[0] = field[last + c_outer]
    e_high[0] = field[c_outer]


def edge_kernel(shape, field, left, right, outer, arrived):
    cells_x, cells_y = shape
    c_outer = (lax.axis_index("gy") % 2) * (cells_y - 1)
    pairs = [(field.at[cells_x - 1], left), (field.at[0], right)]
    pairs += [(field.at[x, c_outer], outer.at[x]) for x in range(cells_x)]
    loads = [pltpu.make_async_copy(*pair, arrived.at[k]) for k, pair in enumerate(pairs)]
    for load in loads:
        load.start()
    for load in loads:
        load.wait()


def first_pack_kernel(shape, field, left, right, done, outer, close):
    cells_x, cells_y = shape
    odd = lax.axis_index("gy") % 2
    c_outer, c_close = odd * (cells_y - 1), (1 - odd) * (cells_y - 1)
    outer[0] = left[c_outer]
    outer[1] = right[c_outer]
    for x in range(cells_x):
        close[x] = field[x * cells_y + c_close]
    close[cells_x] = left[c_close]
    close[cells_x + 1] = right[c_close]


def pack_close_kernel(left, right, outer, low, high, close, done, out):
    near = (1 - lax.axis_index("gy") % 2) * (left.shape[0] - 1)
    cells_x = close.shape[0]
    for x in range(cells_x):
        out[x] = close[x]
    out[cells_x] = left[near]
    out[cells_x + 1] = right[near]


def pack_kernel(scale, first, second, third, out):
    terms = jnp.concatenate([r[k] for r in (first, second, third) for k in range(2)], axis=0)
    ones = jnp.full((8, terms.shape[1]), scale, F32)
    row = lax.dot_general(
        ones, terms, (((1,), (1,)), ((), ())), precision=lax.Precision.HIGHEST, preferred_element_type=F32
    )
    lanes = out.shape[2]
    row = jnp.concatenate([row, jnp.zeros((8, 2 * lanes - row.shape[1]), F32)], axis=1)
    out[:, 0, :] = jnp.broadcast_to(row[0:1, :lanes], (out.shape[0], lanes))
    out[:, 1, :] = jnp.broadcast_to(row[0:1, lanes:], (out.shape[0], lanes))


def params(mib):
    return pltpu.CompilerParams(vmem_limit_bytes=mib << 20)


def shards(sizes, probes, pair_blocks, partners, shifts, counts, kpoint):
    size_x, size_y = sizes
    cells_x, cells_y, width, block = probes.shape
    shape = (cells_x, cells_y)
    slots = pair_blocks.shape[2]
    cells = cells_x * cells_y
    half = width // 2
    total_x, total_y = cells_x * size_x, cells_y * size_y
    def table(move):
        pairs = []
        for i in range(size_x):
            for j in range(size_y):
                a, b = move(i, j)
                pairs.append((i * size_y + j, (a % size_x) * size_y + b % size_y))
        return pairs

    def over(j):
        return j + 1 if j % 2 else j - 1

    moves = [
        table(lambda i, j: (i + 1, j)),
        table(lambda i, j: (i - 1, j)),
        table(lambda i, j: (i, over(j))),
        table(lambda i, j: (i + 1, over(j))),
        table(lambda i, j: (i - 1, over(j))),
    ]
    on_chip = table(lambda i, j: (i, j ^ 1))

    def send(value, move):
        return lax.ppermute(value, AXES, move)

    field = probes.reshape(cells, width, block)
    raw = pair_blocks.reshape(cells, slots, block, block)
    cell = (width, block)
    edge_shapes = [
        jax.ShapeDtypeStruct((n,) + cell, F32) for n in (cells_y, cells_y, cells_x, 1, 1, cells_x)
    ]
    field_shape = jax.ShapeDtypeStruct((cells,) + cell, F32)
    inner_shape = jax.ShapeDtypeStruct(((cells_x - 2) * (cells_y - 2),) + cell, F32)
    sums_shape = jax.ShapeDtypeStruct((2, half, block), F32)
    scratch = [pltpu.VMEM((cells_x + 2, 2 * width, (cells_y + 2) * block), BF16)]

    cells_shape = lambda n: jax.ShapeDtypeStruct((n,) + cell, F32)
    call = lambda body, ins, outs, mib, name, **more: pl.pallas_call(
        body, out_shape=outs, in_specs=[VMEM] * ins, out_specs=[VMEM] * len(outs),
        compiler_params=params(mib), name=name, **more,
    )
    sides = pl.pallas_call(
        lambda *r: edge_kernel(shape, *r),
        out_shape=[cells_shape(cells_y)] * 2 + [cells_shape(cells_x)],
        in_specs=[pl.BlockSpec(memory_space=pl.ANY)], out_specs=[VMEM] * 3,
        scratch_shapes=[pltpu.SemaphoreType.DMA((2 + cells_x,))],
        compiler_params=params(1), name="edges",
    )(pltpu.with_memory_space_constraint(probes.reshape(cells_x, cells_y, width, block), pltpu.HBM))

    blocks, turn = pl.pallas_call(
        lambda *r: split_kernel(sizes, shape, *r),
        out_shape=[
            jax.ShapeDtypeStruct((cells, slots * block, 2 * block), BF16),
            jax.ShapeDtypeStruct((10, half, block), F32),
        ],
        in_specs=[SMEM, SMEM, SMEM, pl.BlockSpec(memory_space=pl.ANY)], out_specs=[VMEM] * 2,
        scratch_shapes=[pltpu.VMEM(raw.shape, F32), pltpu.SemaphoreType.DMA((cells,))],
        compiler_params=params(22), name="split",
        cost_estimate=pl.CostEstimate(flops=4 * raw.size, bytes_accessed=8 * raw.size, transcendentals=0),
    )(kpoint, partners, counts, pltpu.with_memory_space_constraint(raw, pltpu.HBM))

    flops = 8 * width * block * block * slots

    rim = len(rim_cells(shape))

    def cost(cells):
        return pl.CostEstimate(flops=cells * flops, bytes_accessed=0, transcendentals=0)

    def inner(first, field, before, after):
        return call(
            lambda *r: inner_kernel(first, shape, *r), 5, [inner_shape, sums_shape], 6, "inner",
            scratch_shapes=scratch, cost_estimate=cost(16),
        )(field, blocks, probes_flat, before, after)

    def local(field, after):
        return call(
            lambda *r: local_kernel(shape, *r), 3, [cells_shape(rim)], 6, "local",
            scratch_shapes=scratch, cost_estimate=cost(12),
        )(field, blocks, after)

    def outside(first, last, before, parts, halo):
        outs = [field_shape, sums_shape] + ([] if last else edge_shapes)
        return call(
            lambda *r: rim_kernel(first, shape, *r), 7 + len(halo), outs, 6, "rim",
            scratch_shapes=scratch, cost_estimate=cost(8),
        )(turn, blocks, probes_flat, before, *parts, *halo)

    def first_step(field, sides):
        halo = [send(s, m) for s, m in zip(sides, moves)]
        corners, close = call(
            lambda *r: first_pack_kernel(shape, *r), 4, [cells_shape(2), cells_shape(cells_x + 2)], 1,
            "pack_sides",
        )(field, *halo[:2], turn)
        after = corners
        corners, close = send(corners, moves[2]), send(close, on_chip)
        parts = [*inner(True, field, field, halo[2]), *local(field, after)]
        return outside(True, False, field, parts, [*halo, close, corners])

    def step(last, field, before, sides):
        *sides, close = sides
        halo = [send(s, m) for s, m in zip(sides, moves)]
        parts = inner(False, field, before, field)
        (close,) = call(
            pack_close_kernel, 7, [cells_shape(cells_x + 2)], 1, "pack_close"
        )(*halo, close, parts[1])
        after = close
        close = send(close, on_chip)
        parts = [*parts, *local(field, after)]
        left, right, outer, low, high = halo
        return outside(False, last, before, parts, [left, right, outer, close, low, high])

    probes_flat = field
    new, sums, *sides = first_step(field, sides)
    before, field, found = field, new, [sums]
    for n in range(1, 3):
        new, sums, *sides = step(n == 2, field, before, sides)
        before, field = field, new
        found.append(sums)

    scale = 1.0 / math.sqrt(total_x * total_y * block)
    spread = pl.pallas_call(
        lambda *r: pack_kernel(scale, *r),
        out_shape=jax.ShapeDtypeStruct((size_x * size_y, 2, 128), F32),
        in_specs=[VMEM] * 3, out_specs=VMEM, compiler_params=params(2), name="pack",
    )(*found)
    total = jnp.sum(lax.all_to_all(spread, AXES, 0, 0), axis=0).reshape(-1)
    total = total[: 3 * 2 * half].reshape(3, 2, half)
    return field.reshape(probes.shape), total


def solution(mesh):
    sizes = (mesh.shape["gx"], mesh.shape["gy"])
    placed = (
        P("gx", "gy", None, None),
        P("gx", "gy", None, None, None),
        P("gx", "gy", None),
        P(None, "gx", "gy", None),
        P("gx", "gy"),
        P(),
    )
    return jax.shard_map(
        lambda *a: shards(sizes, *a), mesh=mesh, in_specs=placed,
        out_specs=(P("gx", "gy", None, None), P()), check_vma=False,
    )
```

```python
import math

import jax
import jax.numpy as jnp
from jax import lax
from jax.experimental import pallas as pl
from jax.experimental.pallas import tpu as pltpu
from jax.sharding import PartitionSpec as P

AXES = ("gx", "gy")
F32 = jnp.float32
BF16 = jnp.bfloat16
VMEM = pl.BlockSpec(memory_space=pltpu.VMEM)
SMEM = pl.BlockSpec(memory_space=pltpu.SMEM)


def split_kernel(sizes, shape, kpoint, partners, counts, source, out, turn, blocks, arrived):
    cells_x, cells_y = shape
    total_x, total_y = sizes[0] * cells_x, sizes[1] * cells_y
    cells, slots, block, _ = blocks.shape
    loads = [pltpu.make_async_copy(source.at[i], blocks.at[i], arrived.at[i]) for i in range(cells)]
    for load in loads:
        load.start()
    me_x, me_y = lax.axis_index("gx"), lax.axis_index("gy")

    wrap_left = jnp.where(me_x == 0, -1.0, 0.0)
    wrap_right = jnp.where(me_x == sizes[0] - 1, 1.0, 0.0)
    wrap_low = jnp.where(me_y == 0, -1.0, 0.0)
    wrap_high = jnp.where(me_y == sizes[1] - 1, 1.0, 0.0)
    wrap_outer = jnp.where(me_y % 2 == 1, wrap_high, wrap_low)
    zero = jnp.zeros_like(wrap_outer)
    sides = [(wrap_left, zero), (wrap_right, zero), (zero, wrap_outer)]
    sides += [(wrap_left, wrap_outer), (wrap_right, wrap_outer)]
    for k, (along_x, along_y) in enumerate(sides):
        angle = jnp.full(turn.shape[1:], kpoint[0] * along_x + kpoint[1] * along_y, F32)
        turn[2 * k] = jnp.cos(angle)
        turn[2 * k + 1] = jnp.sin(angle)

    reach = 20
    scale = -(-(1 << reach) // total_y)
    assert all(p * scale >> reach == p // total_y for p in range(total_x * total_y))

    def offset(place, start, total):
        step = place - start + 1
        return jnp.where(step < 0, step + total, jnp.where(step > 2, step - total, step))

    def body(i, carry):
        x, y = i // cells_y, i % cells_y
        pltpu.make_async_copy(source.at[i], blocks.at[i], arrived.at[i]).wait()
        live = counts[x, y]
        for s in range(slots):
            partner = partners[x, y, s]
            place_x = lax.shift_right_logical(partner * scale, reach)
            along_x = offset(place_x, me_x * cells_x + x, total_x)
            along_y = offset(partner - place_x * total_y, me_y * cells_y + y, total_y)
            row = pl.multiple_of((along_x * 3 + along_y) * block, block)
            value = jnp.where(s < live, blocks[i, s], 0.0)
            high = value.astype(BF16)
            out[i, pl.ds(row, block), 0:block] = high
            out[i, pl.ds(row, block), block : 2 * block] = (value - high.astype(F32)).astype(BF16)
        return carry

    lax.fori_loop(0, cells, body, 0, unroll=2)


def put(ext, x, y, value):
    rows, block = value.shape
    high = value.astype(BF16)
    lanes = pl.ds(pl.multiple_of(y * block, block), block)
    ext[x, 0:rows, lanes] = high
    ext[x, rows : 2 * rows, lanes] = (value - high.astype(F32)).astype(BF16)


def turned(value, cos, sin):
    half = value.shape[0] // 2
    re, im = value[:half], value[half:]
    return jnp.concatenate([cos * re - sin * im, sin * re + cos * im], axis=0)


def fold(full, rows, block):
    return (full[rows:, block:] + full[rows:, :block]) + (full[:rows, block:] + full[:rows, :block])


def apply_cell(ext, blocks, x, y, cells_y):
    block = blocks.shape[2] // 2
    lanes = pl.ds(pl.multiple_of(y * block, block), 3 * block)
    left = jnp.concatenate([ext[x + d, :, lanes] for d in range(3)], axis=1)
    full = jnp.dot(left, blocks[x * cells_y + y], preferred_element_type=F32)
    return fold(full, ext.shape[1] // 2, block)


def apply_part(ext, blocks, x, y, shape, local):
    cells_x, cells_y = shape
    block = blocks.shape[2] // 2
    left, right = [], []
    for k in range(9):
        a, b = x + k // 3, y + k % 3
        if (1 <= a <= cells_x and 1 <= b <= cells_y) == local:
            left.append(ext[a, :, b * block : (b + 1) * block])
            right.append(blocks[x * cells_y + y, k * block : (k + 1) * block, :])
    full = jnp.dot(
        jnp.concatenate(left, axis=1), jnp.concatenate(right, axis=0), preferred_element_type=F32
    )
    return fold(full, ext.shape[1] // 2, block)


def rim_cells(shape):
    cells_x, cells_y = shape
    return [
        (x, y) for x in range(cells_x) for y in range(cells_y)
        if x in (0, cells_x - 1) or y in (0, cells_y - 1)
    ]


def terms(start, value):
    half = value.shape[0] // 2
    real = start[:half] * value[:half] + start[half:] * value[half:]
    return real, start[:half] * value[half:] - start[half:] * value[:half]


def put_field(ext, field, shape):
    cells_x, cells_y = shape
    for x in range(cells_x):
        for y in range(cells_y):
            put(ext, x + 1, y + 1, field[x * cells_y + y])


def inner_kernel(first, shape, field, blocks, probes, before, done, out, sums, ext):
    cells_x, cells_y = shape
    put_field(ext, field, shape)
    sums[...] = jnp.zeros_like(sums)
    width = cells_y - 2

    def body(k, carry):
        x, y = 1 + k // width, 1 + k % width
        i = x * cells_y + y
        value = apply_cell(ext, blocks, x, y, cells_y)
        if not first:
            value = 2.0 * value - before[i]
        out[k] = value
        real, imag = terms(probes[i], value)
        sums[0] += real
        sums[1] += imag
        return carry

    lax.fori_loop(0, (cells_x - 2) * width, body, 0, unroll=4)


def local_kernel(shape, field, blocks, done, out, ext):
    put_field(ext, field, shape)
    for k, (x, y) in enumerate(rim_cells(shape)):
        out[k] = apply_part(ext, blocks, x, y, shape, True)


def rim_kernel(
    first, shape, turn, blocks, probes, before, inner, inner_sums, local, left, right, outer, close, *rest
):
    cells_x, cells_y = shape
    if first:
        low, *rest = rest
        low, high = low.at[0], low.at[1]
    else:
        low, high, *rest = rest
        low, high = low.at[0], high.at[0]
    new, sums, *sides, ext = rest
    odd = lax.axis_index("gy") % 2
    y_outer, y_close = odd * (cells_y + 1), (1 - odd) * (cells_y + 1)
    for y in range(cells_y):
        put(ext, 0, y + 1, turned(left[y], turn[0], turn[1]))
        put(ext, cells_x + 1, y + 1, turned(right[y], turn[2], turn[3]))
    for x in range(cells_x):
        put(ext, x + 1, y_outer, turned(outer[x], turn[4], turn[5]))
        put(ext, x + 1, y_close, close[x])
    put(ext, 0, y_outer, turned(low[...], turn[6], turn[7]))
    put(ext, cells_x + 1, y_outer, turned(high[...], turn[8], turn[9]))
    put(ext, 0, y_close, turned(close[cells_x], turn[0], turn[1]))
    put(ext, cells_x + 1, y_close, turned(close[cells_x + 1], turn[2], turn[3]))
    width = cells_y - 2
    for k in range((cells_x - 2) * width):
        new[(1 + k // width) * cells_y + 1 + k % width] = inner[k]
    real_sum, imag_sum = inner_sums[0], inner_sums[1]
    for k, (x, y) in enumerate(rim_cells(shape)):
        i = x * cells_y + y
        value = local[k] + apply_part(ext, blocks, x, y, shape, False)
        if not first:
            value = 2.0 * value - before[i]
        new[i] = value
        real, imag = terms(probes[i], value)
        real_sum, imag_sum = real_sum + real, imag_sum + imag
    sums[0] = real_sum
    sums[1] = imag_sum
    if sides:
        edges(shape, odd, new, *sides)


def edges(shape, odd, field, e_left, e_right, e_outer, e_low, e_high, e_close):
    cells_x, cells_y = shape
    last = (cells_x - 1) * cells_y
    c_outer, c_close = odd * (cells_y - 1), (1 - odd) * (cells_y - 1)
    for y in range(cells_y):
        e_left[y] = field[last + y]
        e_right[y] = field[y]
    for x in range(cells_x):
        e_outer[x] = field[x * cells_y + c_outer]
        e_close[x] = field[x * cells_y + c_close]
    e_low[0] = field[last + c_outer]
    e_high[0] = field[c_outer]


def edge_kernel(shape, field, left, right, outer, arrived):
    cells_x, cells_y = shape
    c_outer = (lax.axis_index("gy") % 2) * (cells_y - 1)
    pairs = [(field.at[cells_x - 1], left), (field.at[0], right)]
    pairs += [(field.at[x, c_outer], outer.at[x]) for x in range(cells_x)]
    loads = [pltpu.make_async_copy(*pair, arrived.at[k]) for k, pair in enumerate(pairs)]
    for load in loads:
        load.start()
    for load in loads:
        load.wait()


def first_pack_kernel(shape, field, left, right, done, outer, close):
    cells_x, cells_y = shape
    odd = lax.axis_index("gy") % 2
    c_outer, c_close = odd * (cells_y - 1), (1 - odd) * (cells_y - 1)
    outer[0] = left[c_outer]
    outer[1] = right[c_outer]
    for x in range(cells_x):
        close[x] = field[x * cells_y + c_close]
    close[cells_x] = left[c_close]
    close[cells_x + 1] = right[c_close]


def pack_close_kernel(left, right, outer, low, high, close, done, out):
    near = (1 - lax.axis_index("gy") % 2) * (left.shape[0] - 1)
    cells_x = close.shape[0]
    for x in range(cells_x):
        out[x] = close[x]
    out[cells_x] = left[near]
    out[cells_x + 1] = right[near]


def pack_kernel(scale, first, second, third, out):
    terms = jnp.concatenate([r[k] for r in (first, second, third) for k in range(2)], axis=0)
    ones = jnp.full((8, terms.shape[1]), scale, F32)
    row = lax.dot_general(
        ones, terms, (((1,), (1,)), ((), ())), precision=lax.Precision.HIGHEST, preferred_element_type=F32
    )
    lanes = out.shape[2]
    row = jnp.concatenate([row, jnp.zeros((8, 2 * lanes - row.shape[1]), F32)], axis=1)
    out[:, 0, :] = jnp.broadcast_to(row[0:1, :lanes], (out.shape[0], lanes))
    out[:, 1, :] = jnp.broadcast_to(row[0:1, lanes:], (out.shape[0], lanes))


def params(mib):
    return pltpu.CompilerParams(vmem_limit_bytes=mib << 20)


def shards(sizes, probes, pair_blocks, partners, shifts, counts, kpoint):
    size_x, size_y = sizes
    cells_x, cells_y, width, block = probes.shape
    shape = (cells_x, cells_y)
    slots = pair_blocks.shape[2]
    cells = cells_x * cells_y
    half = width // 2
    total_x, total_y = cells_x * size_x, cells_y * size_y
    def table(move):
        pairs = []
        for i in range(size_x):
            for j in range(size_y):
                a, b = move(i, j)
                pairs.append((i * size_y + j, (a % size_x) * size_y + b % size_y))
        return pairs

    def over(j):
        return j + 1 if j % 2 else j - 1

    moves = [
        table(lambda i, j: (i + 1, j)),
        table(lambda i, j: (i - 1, j)),
        table(lambda i, j: (i, over(j))),
        table(lambda i, j: (i + 1, over(j))),
        table(lambda i, j: (i - 1, over(j))),
    ]
    on_chip = table(lambda i, j: (i, j ^ 1))

    def send(value, move):
        return lax.ppermute(value, AXES, move)

    field = probes.reshape(cells, width, block)
    raw = pair_blocks.reshape(cells, slots, block, block)
    cell = (width, block)
    edge_shapes = [
        jax.ShapeDtypeStruct((n,) + cell, F32) for n in (cells_y, cells_y, cells_x, 1, 1, cells_x)
    ]
    field_shape = jax.ShapeDtypeStruct((cells,) + cell, F32)
    inner_shape = jax.ShapeDtypeStruct(((cells_x - 2) * (cells_y - 2),) + cell, F32)
    sums_shape = jax.ShapeDtypeStruct((2, half, block), F32)
    scratch = [pltpu.VMEM((cells_x + 2, 2 * width, (cells_y + 2) * block), BF16)]

    cells_shape = lambda n: jax.ShapeDtypeStruct((n,) + cell, F32)
    call = lambda body, ins, outs, mib, name, **more: pl.pallas_call(
        body, out_shape=outs, in_specs=[VMEM] * ins, out_specs=[VMEM] * len(outs),
        compiler_params=params(mib), name=name, **more,
    )
    sides = pl.pallas_call(
        lambda *r: edge_kernel(shape, *r),
        out_shape=[cells_shape(cells_y)] * 2 + [cells_shape(cells_x)],
        in_specs=[pl.BlockSpec(memory_space=pl.ANY)], out_specs=[VMEM] * 3,
        scratch_shapes=[pltpu.SemaphoreType.DMA((2 + cells_x,))],
        compiler_params=params(1), name="edges",
    )(pltpu.with_memory_space_constraint(probes.reshape(cells_x, cells_y, width, block), pltpu.HBM))

    blocks, turn = pl.pallas_call(
        lambda *r: split_kernel(sizes, shape, *r),
        out_shape=[
            jax.ShapeDtypeStruct((cells, slots * block, 2 * block), BF16),
            jax.ShapeDtypeStruct((10, half, block), F32),
        ],
        in_specs=[SMEM, SMEM, SMEM, pl.BlockSpec(memory_space=pl.ANY)], out_specs=[VMEM] * 2,
        scratch_shapes=[pltpu.VMEM(raw.shape, F32), pltpu.SemaphoreType.DMA((cells,))],
        compiler_params=params(22), name="split",
        cost_estimate=pl.CostEstimate(flops=4 * raw.size, bytes_accessed=8 * raw.size, transcendentals=0),
    )(kpoint, partners, counts, pltpu.with_memory_space_constraint(raw, pltpu.HBM))

    flops = 8 * width * block * block * slots

    rim = len(rim_cells(shape))

    def cost(cells):
        return pl.CostEstimate(flops=cells * flops, bytes_accessed=0, transcendentals=0)

    def inner(first, field, before, after):
        return call(
            lambda *r: inner_kernel(first, shape, *r), 5, [inner_shape, sums_shape], 6, "inner",
            scratch_shapes=scratch, cost_estimate=cost(16),
        )(field, blocks, probes_flat, before, after)

    def local(field, after):
        return call(
            lambda *r: local_kernel(shape, *r), 3, [cells_shape(rim)], 6, "local",
            scratch_shapes=scratch, cost_estimate=cost(12),
        )(field, blocks, after)

    def outside(first, last, before, parts, halo):
        outs = [field_shape, sums_shape] + ([] if last else edge_shapes)
        return call(
            lambda *r: rim_kernel(first, shape, *r), 7 + len(halo), outs, 6, "rim",
            scratch_shapes=scratch, cost_estimate=cost(8),
        )(turn, blocks, probes_flat, before, *parts, *halo)

    def first_step(field, sides):
        halo = [send(s, m) for s, m in zip(sides, moves)]
        corners, close = call(
            lambda *r: first_pack_kernel(shape, *r), 4, [cells_shape(2), cells_shape(cells_x + 2)], 1,
            "pack_sides",
        )(field, *halo[:2], turn)
        after = corners
        corners, close = send(corners, moves[2]), send(close, on_chip)
        parts = [*inner(True, field, field, halo[2]), *local(field, after)]
        return outside(True, False, field, parts, [*halo, close, corners])

    def step(last, field, before, sides):
        *sides, close = sides
        halo = [send(s, m) for s, m in zip(sides, moves)]
        parts = inner(False, field, before, field)
        (close,) = call(
            pack_close_kernel, 7, [cells_shape(cells_x + 2)], 1, "pack_close"
        )(*halo, close, parts[1])
        after = close
        close = send(close, on_chip)
        parts = [*parts, *local(field, after)]
        left, right, outer, low, high = halo
        return outside(False, last, before, parts, [left, right, outer, close, low, high])

    probes_flat = field
    new, sums, *sides = first_step(field, sides)
    before, field, found = field, new, [sums]
    for n in range(1, 3):
        new, sums, *sides = step(n == 2, field, before, sides)
        before, field = field, new
        found.append(sums)

    scale = 1.0 / math.sqrt(total_x * total_y * block)
    spread = pl.pallas_call(
        lambda *r: pack_kernel(scale, *r),
        out_shape=jax.ShapeDtypeStruct((size_x * size_y, 2, 128), F32),
        in_specs=[VMEM] * 3, out_specs=VMEM, compiler_params=params(2), name="pack",
    )(*found)
    total = jnp.sum(lax.all_to_all(spread, AXES, 0, 0), axis=0).reshape(-1)
    total = total[: 3 * 2 * half].reshape(3, 2, half)
    return field.reshape(probes.shape), total


def solution(mesh):
    sizes = (mesh.shape["gx"], mesh.shape["gy"])
    placed = (
        P("gx", "gy", None, None),
        P("gx", "gy", None, None, None),
        P("gx", "gy", None),
        P(None, "gx", "gy", None),
        P("gx", "gy"),
        P(),
    )
    return jax.shard_map(
        lambda *a: shards(sizes, *a), mesh=mesh, in_specs=placed,
        out_specs=(P("gx", "gy", None, None), P()), check_vma=False,
    )
```
